32 devices in a mesh: band: 8 (over z, core), blk: 4 (over y, x).
Axes of the slice: x: 2, y: 2, z: 4, core: 2. Of those that a mesh axis runs over, the one named last changes fastest.
Arguments:
- steering: bfloat16 [4, 6144, 512], P('blk', 'band'), may hold values from -1.4 to 1.4
- estimates: bfloat16 [4, 6144], P('blk', 'band'), may hold values from 0 to 1
- spectra: float32 [4, 256, 512], P('blk', 'band'), may hold values from -768 to 4160
Outputs:
- updated: float32 [4, 6144], P('blk', 'band')
- broadband: float32 [6144], P('band')
The draws below stay inside these ranges and needn't reach their ends.
All inputs are finite; a program needn't handle non-finite values.
Results may differ from the reference program's by a relative error of at most 0.0003.
Values may be sent and summed in bfloat16 or wider, within the bound.
A program may use at most 192 MiB of HBM per device.

```python
import math
import jax
import jax.numpy as jnp
from jax import lax

CHANNELS = 256
GRID_DEV = 768
GRID = 6144
BANDS = 4


def draw_steering(key, part):
    phase_key = jax.random.fold_in(key, 11)
    level_key = jax.random.fold_in(key, 12)
    shape = (BANDS, GRID, CHANNELS)
    phase = jax.random.uniform(phase_key, shape, jnp.float32, -math.pi, math.pi)
    amplitude = jnp.exp(jax.random.uniform(level_key, shape, jnp.float32, math.log(0.7), math.log(1.4)))
    result = jnp.concatenate([amplitude * jnp.cos(phase), amplitude * jnp.sin(phase)], axis=2)
    return result.astype(jnp.bfloat16)


def draw_spectra(key, part):
    noise_key = jax.random.fold_in(key, 21)
    level_key = jax.random.fold_in(key, 22)
    shape = (BANDS, CHANNELS, 2 * CHANNELS)
    noise = jnp.clip(jax.random.normal(noise_key, shape, jnp.float32), -3.0, 3.0)
    noise = noise * CHANNELS
    rows = lax.broadcasted_iota(jnp.int32, (CHANNELS, 2 * CHANNELS), 0)
    columns = lax.broadcasted_iota(jnp.int32, (CHANNELS, 2 * CHANNELS), 1)
    band_keys = jax.random.split(level_key, BANDS)
    order = jax.vmap(lambda one_key: jax.random.permutation(one_key, CHANNELS))(band_keys)
    fraction = order.astype(jnp.float32) * 4.0 / (CHANNELS - 1)
    level = ((9.0 + fraction) * ((CHANNELS + GRID) // 20)).reshape(BANDS, CHANNELS, 1)
    result = jnp.where(rows == columns, level, jnp.where(columns == rows + CHANNELS, 0.0, noise))
    return result.astype(jnp.float32)


def block_levels(own_key, extent, pieces, least, largest):
    level, own = 1.0, jax.random.fold_in(own_key, 6)
    for position, parts in pieces:
        heights = jnp.exp(jax.random.uniform(jax.random.fold_in(own, position), (parts,), jnp.float32, least / len(pieces), largest / len(pieces)))
        level = level * jnp.repeat(heights, extent[position] // parts).reshape([-1 if axis == position else 1 for axis in range(len(extent))])
    return level


def setup_inputs(seed: int = 0) -> dict:
    keys = jax.random.split(jax.random.key(seed), 4)
    steering = draw_steering(jax.random.fold_in(keys[3], 71), 0)
    estimates = jnp.clip(1.0 * jax.random.uniform(keys[1], (BANDS, GRID), jnp.float32) ** block_levels(keys[1], (BANDS, GRID), ((0, 4), (1, 8)), -0.2, 0.2), 0.0, 1.0).astype(jnp.bfloat16)
    spectra = draw_spectra(jax.random.fold_in(keys[3], 71), 0)
    return {"steering": steering, "estimates": estimates, "spectra": spectra}


def beam_map(steer_wide, cross):
    width = CHANNELS
    cross_real = cross[:, :width]
    cross_imag = cross[:, width:]
    kernel_real = jnp.concatenate([cross_real, -cross_imag], axis=1)
    kernel_imag = jnp.concatenate([cross_imag, cross_real], axis=1)
    real_part = jnp.dot(steer_wide, kernel_real.T, precision=lax.Precision.HIGHEST, preferred_element_type=jnp.float32)
    imag_part = jnp.dot(steer_wide, kernel_imag.T, precision=lax.Precision.HIGHEST, preferred_element_type=jnp.float32)
    summed = jnp.sum(steer_wide[:, :width] * real_part + steer_wide[:, width:] * imag_part, axis=1)
    return summed / (width * width)


def band_update(operands):
    steering, estimates, spectra = operands
    width = CHANNELS
    steer_wide = steering.astype(jnp.float32)
    beam = beam_map(steer_wide, spectra)
    turned = jnp.concatenate([-steering[:, width:], steering[:, :width]], axis=1)
    values = estimates.astype(jnp.float32)
    blocks = steering.reshape(GRID // GRID_DEV, GRID_DEV, 2 * width)
    turned_blocks = turned.reshape(GRID // GRID_DEV, GRID_DEV, 2 * width)

    def one_block(pair):
        rows, turned_rows = pair
        real_sum = jnp.dot(rows, steering.T, preferred_element_type=jnp.float32)
        imag_sum = jnp.dot(turned_rows, steering.T, preferred_element_type=jnp.float32)
        tile = (real_sum * real_sum + imag_sum * imag_sum) / (width * width)
        return jnp.dot(tile, values, precision=lax.Precision.HIGHEST, preferred_element_type=jnp.float32)

    applied = lax.map(one_block, (blocks, turned_blocks)).reshape(GRID)
    power = jnp.sum(steer_wide * steer_wide, axis=1)
    diag = power * power / (width * width)
    return jnp.maximum(values + (beam - applied) / diag, 0.0)


def reference(steering, estimates, spectra):
    updated = lax.map(band_update, (steering, estimates, spectra))
    return updated, jnp.sum(updated, axis=0)
```

```python
import functools

import jax
import jax.numpy as jnp
from jax import lax
from jax.experimental import pallas as pl
from jax.experimental.pallas import tpu as pltpu
from jax.sharding import PartitionSpec as P

MESH = pl.DeviceIdType.MESH
F32 = jnp.float32
BF16 = jnp.bfloat16


def split(value):
    high = value.astype(BF16)
    low = (value - high.astype(F32)).astype(BF16)
    return jnp.concatenate([high, low], axis=0)


def kernel(
    n, nb, s_ref, x_ref, c_ref, up_ref, bb_ref, t_ref, z_ref, a_ref, b_ref, pair_ref, mine_ref, part_ref, block_ref, d_ref, blk_ref,
    pair_send, pair_recv, part_send, part_recv, ring_send, ring_recv, over_send, over_recv, blk_send, blk_recv,
):
    me, group = lax.axis_index("band"), lax.axis_index("blk")
    chips = n // 2
    chip, core = me // 2, me % 2
    partner = chip * 2 + (1 - core)
    rows, width = c_ref.shape[0], c_ref.shape[1] // 2
    half = width // 2
    piece = half // chips
    others = [(chip + step) % chips for step in range(1, chips)]
    peers = [(group + step) % nb for step in range(1, nb)]

    barrier = pltpu.get_barrier_semaphore()
    pl.semaphore_signal(barrier, inc=1, device_id={"band": partner}, device_id_type=MESH)
    for other in others:
        pl.semaphore_signal(barrier, inc=1, device_id={"band": other * 2 + core}, device_id_type=MESH)
    for peer in peers:
        pl.semaphore_signal(barrier, inc=1, device_id={"blk": peer}, device_id_type=MESH)

    real, imag = c_ref[:, :width], c_ref[:, width:]
    t_ref[...] = jnp.zeros_like(t_ref)
    z_ref[...] = jnp.zeros_like(z_ref)
    within = pl.multiple_of((me % chips) * rows, rows)
    z_ref[pl.ds(within, rows), :] = (real + imag) * 0.5
    t_ref[:, pl.ds(pl.multiple_of((me // chips) * half, half), half)] = z_ref[...].T
    t_ref[pl.ds(pl.multiple_of(me * rows, rows), rows), :] += (real - imag) * 0.5

    x = x_ref[...].astype(F32)

    def build(side):
        at = pl.multiple_of(side * half, half)
        a_half = s_ref[:, pl.ds(at, half)].T
        b_half = s_ref[:, pl.ds(pl.multiple_of(width + side * half, half), half)].T
        a_ref[pl.ds(at, half), :] = a_half
        b_ref[pl.ds(at, half), :] = b_half
        a_wide, b_wide = a_half.astype(F32), b_half.astype(F32)
        total = jnp.dot(split(x * (a_wide - b_wide)), s_ref[:, :width], preferred_element_type=F32)
        total += jnp.dot(split(x * (a_wide + b_wide)), s_ref[:, width:], preferred_element_type=F32)
        return t_ref[pl.ds(at, half), :] - (total[:half] + total[half:])

    theirs = pl.multiple_of((1 - core) * half, half)
    t_ref[pl.ds(theirs, half), :] = build(1 - core)
    pl.semaphore_wait(barrier, 1 + len(others) + len(peers))
    swap = pltpu.make_async_remote_copy(
        src_ref=t_ref.at[pl.ds(theirs, half), :],
        dst_ref=pair_ref,
        send_sem=pair_send,
        recv_sem=pair_recv,
        device_id={"band": partner},
        device_id_type=MESH,
    )
    swap.start()
    own = build(core)
    swap.wait_recv()
    mine_ref[...] = (own + pair_ref[...]).reshape(mine_ref.shape)

    sends = []
    for step, other in enumerate(others):
        copy = pltpu.make_async_remote_copy(
            src_ref=mine_ref.at[other],
            dst_ref=part_ref.at[step],
            send_sem=part_send.at[step],
            recv_sem=part_recv.at[step],
            device_id={"band": other * 2 + core},
            device_id_type=MESH,
        )
        copy.start()
        sends.append(copy)

    a_wide, b_wide = a_ref[...].astype(F32), b_ref[...].astype(F32)
    power = jnp.sum(a_wide * a_wide + b_wide * b_wide, axis=0, keepdims=True)
    swap.wait_send()

    total = mine_ref[chip]
    for step in range(chips - 1):
        sends[step].wait_recv()
        total += part_ref[step]
    block_ref[...] = total

    def place(which, side):
        return pl.ds(pl.multiple_of(side * half + which * piece, piece), piece)

    gathers, handed = [], []

    def hand_over(index, source, which):
        copy = pltpu.make_async_remote_copy(
            src_ref=source,
            dst_ref=d_ref.at[place(which, core), :],
            send_sem=over_send.at[index],
            recv_sem=over_recv.at[index],
            device_id={"band": partner},
            device_id_type=MESH,
        )
        copy.start()
        handed.append(copy)

    for step, other in enumerate(others):
        copy = pltpu.make_async_remote_copy(
            src_ref=block_ref,
            dst_ref=d_ref.at[place(chip, core), :],
            send_sem=ring_send.at[step],
            recv_sem=ring_recv.at[step],
            device_id={"band": other * 2 + core},
            device_id_type=MESH,
        )
        copy.start()
        gathers.append(copy)
    hand_over(chips - 1, block_ref, chip)
    d_ref[place(chip, core), :] = total
    for step in range(chips - 1):
        gathers[step].wait_recv()
        source = (chip + chips - 1 - step) % chips
        hand_over(step, d_ref.at[place(source, core), :], source)
    for copy in handed:
        copy.wait_recv()

    d = split(d_ref[...])
    u = jnp.dot(d, a_ref[...], preferred_element_type=F32)
    v = jnp.dot(d, b_ref[...], preferred_element_type=F32)
    u, v = u[:width] + u[width:], v[:width] + v[width:]
    residual = jnp.sum(u * (a_wide - b_wide) + v * (a_wide + b_wide), axis=0, keepdims=True) / (width * width)
    updated = jnp.maximum(x + residual / (power * power / (width * width)), 0.0)
    up_ref[...] = updated
    blk_ref[group] = updated

    exchanges = []
    for step, peer in enumerate(peers):
        copy = pltpu.make_async_remote_copy(
            src_ref=blk_ref.at[group],
            dst_ref=blk_ref.at[group],
            send_sem=blk_send.at[step],
            recv_sem=blk_recv.at[step],
            device_id={"blk": peer},
            device_id_type=MESH,
        )
        copy.start()
        exchanges.append(copy)
    for copy in sends + gathers + handed:
        copy.wait_send()
    for copy in exchanges:
        copy.wait_recv()
    broad = blk_ref[0]
    for index in range(1, nb):
        broad += blk_ref[index]
    bb_ref[...] = broad
    for copy in exchanges:
        copy.wait_send()


def body(n, nb, steering, estimates, spectra):
    points, doubled = steering.shape[1:]
    width = doubled // 2
    chips, half = n // 2, width // 2
    dma = pltpu.SemaphoreType.DMA
    updated, broadband = pl.pallas_call(
        functools.partial(kernel, n, nb),
        out_shape=[jax.ShapeDtypeStruct((1, points), F32), jax.ShapeDtypeStruct((1, points), F32)],
        in_specs=[pl.BlockSpec(memory_space=pltpu.VMEM)] * 3,
        out_specs=[pl.BlockSpec(memory_space=pltpu.VMEM)] * 2,
        scratch_shapes=[
            pltpu.VMEM((width, width), F32),
            pltpu.VMEM((half, width), F32),
            pltpu.VMEM((width, points), BF16),
            pltpu.VMEM((width, points), BF16),
            pltpu.VMEM((half, width), F32),
            pltpu.VMEM((chips, half // chips, width), F32),
            pltpu.VMEM((chips - 1, half // chips, width), F32),
            pltpu.VMEM((half // chips, width), F32),
            pltpu.VMEM((width, width), F32),
            pltpu.VMEM((nb, 1, points), F32),
            dma, dma,
            dma((chips - 1,)), dma((chips - 1,)),
            dma((chips - 1,)), dma((chips - 1,)),
            dma((chips,)), dma((chips,)),
            dma((nb - 1,)), dma((nb - 1,)),
        ],
        compiler_params=pltpu.CompilerParams(collective_id=0, has_side_effects=True),
    )(steering[0], estimates, spectra[0])
    return updated, broadband.reshape(points)


def solution(mesh):
    return jax.shard_map(
        functools.partial(body, mesh.shape["band"], mesh.shape["blk"]),
        mesh=mesh,
        in_specs=(P("blk", "band", None), P("blk", "band"), P("blk", "band", None)),
        out_specs=(P("blk", "band"), P("band")),
        check_vma=False,
    )
```

```python
import functools

import jax
import jax.numpy as jnp
from jax import lax
from jax.experimental import pallas as pl
from jax.experimental.pallas import tpu as pltpu
from jax.sharding import PartitionSpec as P

MESH = pl.DeviceIdType.MESH
F32 = jnp.float32
BF16 = jnp.bfloat16


def split(value):
    high = value.astype(BF16)
    low = (value - high.astype(F32)).astype(BF16)
    return jnp.concatenate([high, low], axis=0)


def kernel(
    n, nb, chunks, s_hbm, x_hbm, c_hbm, out_ref, s_ref, x_ref, c_ref, t_ref, z_ref, a_ref, b_ref, pair_ref, mine_ref, in_ref, d_ref,
    blk_ref, load_sem, pair_send, pair_recv, go_send, go_recv, all_send, all_recv, over_send, over_recv, blk_send, blk_recv,
):
    me, group = lax.axis_index("band"), lax.axis_index("blk")
    chips = n // 2
    chip, core = me // 2, me % 2
    partner = chip * 2 + (1 - core)
    rows, width = c_ref.shape[0], c_ref.shape[1] // 2
    half = width // 2
    piece = half // chunks
    first = chips // 2 - 1
    others = [(chip + step) % chips for step in range(1, chips)]
    peers = [(group + step) % nb for step in range(1, nb)]

    barrier = pltpu.get_barrier_semaphore()
    pl.semaphore_signal(barrier, inc=1, device_id={"band": partner}, device_id_type=MESH)
    for other in others:
        pl.semaphore_signal(barrier, inc=1, device_id={"band": other * 2 + core}, device_id_type=MESH)
    for peer in peers:
        pl.semaphore_signal(barrier, inc=1, device_id={"blk": peer}, device_id_type=MESH)
    loads = [
        pltpu.make_async_copy(source, target, load_sem.at[index])
        for index, (source, target) in enumerate(((c_hbm, c_ref), (x_hbm, x_ref), (s_hbm, s_ref)))
    ]
    for load in loads:
        load.start()

    t_ref[...] = jnp.zeros_like(t_ref)
    z_ref[...] = jnp.zeros_like(z_ref)
    loads[0].wait()
    real, imag = c_ref[:, :width], c_ref[:, width:]
    within = pl.multiple_of((me % chips) * rows, rows)
    z_ref[pl.ds(within, rows), :] = (real + imag) * 0.5
    t_ref[:, pl.ds(pl.multiple_of((me // chips) * half, half), half)] = z_ref[...].T
    t_ref[pl.ds(pl.multiple_of(me * rows, rows), rows), :] += (real - imag) * 0.5
    loads[1].wait()
    x = x_ref[...].astype(F32)
    loads[2].wait()

    def build(side):
        at = pl.multiple_of(side * half, half)
        a_half = s_ref[:, pl.ds(at, half)].T
        b_half = s_ref[:, pl.ds(pl.multiple_of(width + side * half, half), half)].T
        a_ref[pl.ds(at, half), :] = a_half
        b_ref[pl.ds(at, half), :] = b_half
        a_wide, b_wide = a_half.astype(F32), b_half.astype(F32)
        total = jnp.dot(split(x * (a_wide - b_wide)), s_ref[:, :width], preferred_element_type=F32)
        total += jnp.dot(split(x * (a_wide + b_wide)), s_ref[:, width:], preferred_element_type=F32)
        return t_ref[pl.ds(at, half), :] - (total[:half] + total[half:])

    pair_ref[0] = build(1 - core).reshape(chunks, piece, width)

    pl.semaphore_wait(barrier, 1 + len(others) + len(peers))

    swaps = []
    for j in range(chunks):
        copy = pltpu.make_async_remote_copy(
            src_ref=pair_ref.at[0, j],
            dst_ref=pair_ref.at[1, j],
            send_sem=pair_send.at[j],
            recv_sem=pair_recv.at[j],
            device_id={"band": partner},
            device_id_type=MESH,
        )
        copy.start()
        swaps.append(copy)
    mine_ref[...] = build(core).reshape(mine_ref.shape)

    per = chunks // 2
    order = [(owner, owner * per + j) for j in range(per) for owner in range(2)]

    def to_owner(owner, j):
        return pltpu.make_async_remote_copy(
            src_ref=mine_ref.at[j],
            dst_ref=in_ref.at[chip, j % per],
            send_sem=go_send.at[j],
            recv_sem=go_recv.at[chip, j % per],
            device_id={"band": (first + owner) * 2 + core},
            device_id_type=MESH,
        )

    def from_chip(other, j):
        return pltpu.make_async_remote_copy(
            src_ref=mine_ref.at[j],
            dst_ref=in_ref.at[other, j % per],
            send_sem=go_send.at[j],
            recv_sem=go_recv.at[other, j % per],
            device_id={"band": other * 2 + core},
            device_id_type=MESH,
        )

    def spread(step, j):
        return pltpu.make_async_remote_copy(
            src_ref=d_ref.at[core, j],
            dst_ref=d_ref.at[core, j],
            send_sem=all_send.at[step, j],
            recv_sem=all_recv.at[j],
            device_id={"band": others[step] * 2 + core},
            device_id_type=MESH,
        )

    def hand_over(j):
        return pltpu.make_async_remote_copy(
            src_ref=d_ref.at[core, j],
            dst_ref=d_ref.at[core, j],
            send_sem=over_send.at[j],
            recv_sem=over_recv.at[j],
            device_id={"band": partner},
            device_id_type=MESH,
        )

    for owner, j in order:
        swaps[j].wait_recv()
        mine_ref[j] += pair_ref[1, j]

        @pl.when(chip != first + owner)
        def _():
            to_owner(owner, j).start()

    for owner in range(2):

        @pl.when(chip == first + owner)
        def _():
            for j in range(owner * per, owner * per + per):
                total = mine_ref[j]
                for other in others:
                    from_chip(other, j).wait_recv()
                    total += in_ref[other, j % per]
                d_ref[core, j] = total
                for step in range(chips - 1):
                    spread(step, j).start()
                hand_over(j).start()

    for owner, j in order:

        @pl.when(chip != first + owner)
        def _():
            spread(0, j).wait_recv()
            hand_over(j).start()

    def quadratic(side):
        at = pl.ds(pl.multiple_of(side * half, half), half)
        d = split(d_ref[side].reshape(half, width))
        u = jnp.dot(d, a_ref[...], preferred_element_type=F32)
        v = jnp.dot(d, b_ref[...], preferred_element_type=F32)
        u, v = u[:half] + u[half:], v[:half] + v[half:]
        a_wide, b_wide = a_ref[at, :].astype(F32), b_ref[at, :].astype(F32)
        return jnp.sum(u * (a_wide - b_wide) + v * (a_wide + b_wide), axis=0, keepdims=True)

    a_wide, b_wide = a_ref[...].astype(F32), b_ref[...].astype(F32)
    power = jnp.sum(a_wide * a_wide + b_wide * b_wide, axis=0, keepdims=True)
    residual = quadratic(core)
    for j in range(chunks):
        hand_over(j).wait_recv()
    residual = (residual + quadratic(1 - core)) / (width * width)
    updated = jnp.maximum(x + residual / (power * power / (width * width)), 0.0)
    blk_ref[group] = updated

    exchanges = []
    for step, peer in enumerate(peers):
        copy = pltpu.make_async_remote_copy(
            src_ref=blk_ref.at[group],
            dst_ref=blk_ref.at[group],
            send_sem=blk_send.at[step],
            recv_sem=blk_recv.at[step],
            device_id={"blk": peer},
            device_id_type=MESH,
        )
        copy.start()
        exchanges.append(copy)
    out_ref[0:1, :] = updated
    for copy in swaps:
        copy.wait_send()
    for owner, j in order:
        hand_over(j).wait_send()

        @pl.when(chip != first + owner)
        def _():
            to_owner(owner, j).wait_send()

        @pl.when(chip == first + owner)
        def _():
            for step in range(chips - 1):
                spread(step, j).wait_send()

    for copy in exchanges:
        copy.wait_recv()
    broad = blk_ref[0]
    for index in range(1, nb):
        broad += blk_ref[index]
    out_ref[1:2, :] = broad
    for copy in exchanges:
        copy.wait_send()


def store(both_ref, up_ref, bb_ref):
    up_ref[...] = both_ref[0:1, :]
    bb_ref[...] = both_ref[1:2, :].reshape(bb_ref.shape)


CHUNKS = 4


def body(n, nb, steering, estimates, spectra):
    points, doubled = steering.shape[1:]
    rows, width = spectra.shape[1], doubled // 2
    half, chunks = width // 2, CHUNKS
    piece = half // chunks
    dma = pltpu.SemaphoreType.DMA
    both = pl.pallas_call(
        functools.partial(kernel, n, nb, chunks),
        out_shape=jax.ShapeDtypeStruct((2, points), F32),
        in_specs=[pl.BlockSpec(memory_space=pltpu.HBM)] * 3,
        out_specs=pl.BlockSpec(memory_space=pltpu.VMEM),
        scratch_shapes=[
            pltpu.VMEM((points, doubled), BF16),
            pltpu.VMEM((1, points), BF16),
            pltpu.VMEM((rows, doubled), F32),
            pltpu.VMEM((width, width), F32),
            pltpu.VMEM((half, width), F32),
            pltpu.VMEM((width, points), BF16),
            pltpu.VMEM((width, points), BF16),
            pltpu.VMEM((2, chunks, piece, width), F32),
            pltpu.VMEM((chunks, piece, width), F32),
            pltpu.VMEM((n // 2, chunks // 2, piece, width), F32),
            pltpu.VMEM((2, chunks, piece, width), F32),
            pltpu.VMEM((nb, 1, points), F32),
            dma((3,)),
            dma((chunks,)), dma((chunks,)),
            dma((chunks,)), dma((n // 2, chunks // 2)),
            dma((n // 2 - 1, chunks)), dma((chunks,)),
            dma((chunks,)), dma((chunks,)),
            dma((nb - 1,)), dma((nb - 1,)),
        ],
        compiler_params=pltpu.CompilerParams(collective_id=0, has_side_effects=True, vmem_limit_bytes=60 * 2**20),
    )(steering[0], estimates, spectra[0])
    updated, broadband = pl.pallas_call(
        store,
        out_shape=[jax.ShapeDtypeStruct((1, points), F32), jax.ShapeDtypeStruct((points,), F32)],
        in_specs=[pl.BlockSpec(memory_space=pltpu.VMEM)],
        out_specs=[pl.BlockSpec(memory_space=pltpu.VMEM)] * 2,
        compiler_params=pltpu.CompilerParams(vmem_limit_bytes=4 * 2**20),
    )(both)
    return updated, broadband


def solution(mesh):
    return jax.shard_map(
        functools.partial(body, mesh.shape["band"], mesh.shape["blk"]),
        mesh=mesh,
        in_specs=(P("blk", "band", None), P("blk", "band"), P("blk", "band", None)),
        out_specs=(P("blk", "band"), P("band")),
        check_vma=False,
    )
```

```python
import functools

import jax
import jax.numpy as jnp
from jax import lax
from jax.experimental import pallas as pl
from jax.experimental.pallas import tpu as pltpu
from jax.sharding import PartitionSpec as P

MESH = pl.DeviceIdType.MESH
F32 = jnp.float32
BF16 = jnp.bfloat16


def split(value):
    high = value.astype(BF16)
    low = (value - high.astype(F32)).astype(BF16)
    return jnp.concatenate([high, low], axis=0)


def kernel(
    n, nb, chunks, s_hbm, x_hbm, c_hbm, out_ref, s_ref, x_ref, c_ref, t_ref, z_ref, a_ref, b_ref, pair_ref, mine_ref, in_ref, d_ref,
    blk_ref, load_sem, pair_send, pair_recv, go_send, go_recv, all_send, all_recv, over_send, over_recv, blk_send, blk_recv,
):
    me, group = lax.axis_index("band"), lax.axis_index("blk")
    chips = n // 2
    chip, core = me // 2, me % 2
    partner = chip * 2 + (1 - core)
    rows, width = c_ref.shape[0], c_ref.shape[1] // 2
    half = width // 2
    piece = half // chunks
    first = chips // 2 - 1
    others = [(chip + step) % chips for step in range(1, chips)]
    peers = [(group + step) % nb for step in range(1, nb)]

    barrier = pltpu.get_barrier_semaphore()
    pl.semaphore_signal(barrier, inc=1, device_id={"band": partner}, device_id_type=MESH)
    for other in others:
        pl.semaphore_signal(barrier, inc=1, device_id={"band": other * 2 + core}, device_id_type=MESH)
    for peer in peers:
        pl.semaphore_signal(barrier, inc=1, device_id={"blk": peer}, device_id_type=MESH)
    loads = [
        pltpu.make_async_copy(source, target, load_sem.at[index])
        for index, (source, target) in enumerate(((c_hbm, c_ref), (x_hbm, x_ref), (s_hbm, s_ref)))
    ]
    for load in loads:
        load.start()

    t_ref[...] = jnp.zeros_like(t_ref)
    z_ref[...] = jnp.zeros_like(z_ref)
    loads[0].wait()
    real, imag = c_ref[:, :width], c_ref[:, width:]
    within = pl.multiple_of((me % chips) * rows, rows)
    z_ref[pl.ds(within, rows), :] = (real + imag) * 0.5
    t_ref[:, pl.ds(pl.multiple_of((me // chips) * half, half), half)] = z_ref[...].T
    t_ref[pl.ds(pl.multiple_of(me * rows, rows), rows), :] += (real - imag) * 0.5
    loads[1].wait()
    x = x_ref[...].astype(F32)
    loads[2].wait()

    def build(side):
        at = pl.multiple_of(side * half, half)
        a_half = s_ref[:, pl.ds(at, half)].T
        b_half = s_ref[:, pl.ds(pl.multiple_of(width + side * half, half), half)].T
        a_ref[pl.ds(at, half), :] = a_half
        b_ref[pl.ds(at, half), :] = b_half
        a_wide, b_wide = a_half.astype(F32), b_half.astype(F32)
        total = jnp.dot(split(x * (a_wide - b_wide)), s_ref[:, :width], preferred_element_type=F32)
        total += jnp.dot(split(x * (a_wide + b_wide)), s_ref[:, width:], preferred_element_type=F32)
        return t_ref[pl.ds(at, half), :] - (total[:half] + total[half:])

    pair_ref[0] = build(1 - core).reshape(chunks, piece, width)

    pl.semaphore_wait(barrier, 1 + len(others) + len(peers))

    swaps = []
    for j in range(chunks):
        copy = pltpu.make_async_remote_copy(
            src_ref=pair_ref.at[0, j],
            dst_ref=pair_ref.at[1, j],
            send_sem=pair_send.at[j],
            recv_sem=pair_recv.at[j],
            device_id={"band": partner},
            device_id_type=MESH,
        )
        copy.start()
        swaps.append(copy)
    mine_ref[...] = build(core).reshape(mine_ref.shape)

    per = chunks // 2
    order = [(owner, owner * per + j) for j in range(per) for owner in range(2)]

    def to_owner(owner, j):
        return pltpu.make_async_remote_copy(
            src_ref=mine_ref.at[j],
            dst_ref=in_ref.at[chip, j % per],
            send_sem=go_send.at[j],
            recv_sem=go_recv.at[chip, j % per],
            device_id={"band": (first + owner) * 2 + core},
            device_id_type=MESH,
        )

    def from_chip(other, j):
        return pltpu.make_async_remote_copy(
            src_ref=mine_ref.at[j],
            dst_ref=in_ref.at[other, j % per],
            send_sem=go_send.at[j],
            recv_sem=go_recv.at[other, j % per],
            device_id={"band": other * 2 + core},
            device_id_type=MESH,
        )

    def spread(step, j):
        return pltpu.make_async_remote_copy(
            src_ref=d_ref.at[core, j],
            dst_ref=d_ref.at[core, j],
            send_sem=all_send.at[step, j],
            recv_sem=all_recv.at[j],
            device_id={"band": others[step] * 2 + core},
            device_id_type=MESH,
        )

    def hand_over(j):
        return pltpu.make_async_remote_copy(
            src_ref=d_ref.at[core, j],
            dst_ref=d_ref.at[core, j],
            send_sem=over_send.at[j],
            recv_sem=over_recv.at[j],
            device_id={"band": partner},
            device_id_type=MESH,
        )

    for owner, j in order:
        swaps[j].wait_recv()
        mine_ref[j] += pair_ref[1, j]

        @pl.when(chip != first + owner)
        def _():
            to_owner(owner, j).start()

    for owner in range(2):

        @pl.when(chip == first + owner)
        def _():
            for j in range(owner * per, owner * per + per):
                total = mine_ref[j]
                for other in others:
                    from_chip(other, j).wait_recv()
                    total += in_ref[other, j % per]
                d_ref[core, j] = total
                for step in range(chips - 1):
                    spread(step, j).start()
                hand_over(j).start()

    for owner, j in order:

        @pl.when(chip != first + owner)
        def _():
            spread(0, j).wait_recv()
            hand_over(j).start()

    def quadratic(side):
        at = pl.ds(pl.multiple_of(side * half, half), half)
        d = split(d_ref[side].reshape(half, width))
        u = jnp.dot(d, a_ref[...], preferred_element_type=F32)
        v = jnp.dot(d, b_ref[...], preferred_element_type=F32)
        u, v = u[:half] + u[half:], v[:half] + v[half:]
        a_wide, b_wide = a_ref[at, :].astype(F32), b_ref[at, :].astype(F32)
        return jnp.sum(u * (a_wide - b_wide) + v * (a_wide + b_wide), axis=0, keepdims=True)

    a_wide, b_wide = a_ref[...].astype(F32), b_ref[...].astype(F32)
    power = jnp.sum(a_wide * a_wide + b_wide * b_wide, axis=0, keepdims=True)
    residual = quadratic(core)
    for j in range(chunks):
        hand_over(j).wait_recv()
    residual = (residual + quadratic(1 - core)) / (width * width)
    updated = jnp.maximum(x + residual / (power * power / (width * width)), 0.0)
    blk_ref[group] = updated

    exchanges = []
    for step, peer in enumerate(peers):
        copy = pltpu.make_async_remote_copy(
            src_ref=blk_ref.at[group],
            dst_ref=blk_ref.at[group],
            send_sem=blk_send.at[step],
            recv_sem=blk_recv.at[step],
            device_id={"blk": peer},
            device_id_type=MESH,
        )
        copy.start()
        exchanges.append(copy)
    out_ref[0:1, :] = updated
    for copy in swaps:
        copy.wait_send()
    for owner, j in order:
        hand_over(j).wait_send()

        @pl.when(chip != first + owner)
        def _():
            to_owner(owner, j).wait_send()

        @pl.when(chip == first + owner)
        def _():
            for step in range(chips - 1):
                spread(step, j).wait_send()

    for copy in exchanges:
        copy.wait_recv()
    broad = blk_ref[0]
    for index in range(1, nb):
        broad += blk_ref[index]
    out_ref[1:2, :] = broad
    for copy in exchanges:
        copy.wait_send()


def store(both_ref, up_ref, bb_ref):
    up_ref[...] = both_ref[0:1, :]
    bb_ref[...] = both_ref[1:2, :].reshape(bb_ref.shape)


CHUNKS = 4


def body(n, nb, steering, estimates, spectra):
    points, doubled = steering.shape[1:]
    rows, width = spectra.shape[1], doubled // 2
    half, chunks = width // 2, CHUNKS
    piece = half // chunks
    dma = pltpu.SemaphoreType.DMA
    both = pl.pallas_call(
        functools.partial(kernel, n, nb, chunks),
        out_shape=jax.ShapeDtypeStruct((2, points), F32),
        in_specs=[pl.BlockSpec(memory_space=pltpu.HBM)] * 3,
        out_specs=pl.BlockSpec(memory_space=pltpu.VMEM),
        scratch_shapes=[
            pltpu.VMEM((points, doubled), BF16),
            pltpu.VMEM((1, points), BF16),
            pltpu.VMEM((rows, doubled), F32),
            pltpu.VMEM((width, width), F32),
            pltpu.VMEM((half, width), F32),
            pltpu.VMEM((width, points), BF16),
            pltpu.VMEM((width, points), BF16),
            pltpu.VMEM((2, chunks, piece, width), F32),
            pltpu.VMEM((chunks, piece, width), F32),
            pltpu.VMEM((n // 2, chunks // 2, piece, width), F32),
            pltpu.VMEM((2, chunks, piece, width), F32),
            pltpu.VMEM((nb, 1, points), F32),
            dma((3,)),
            dma((chunks,)), dma((chunks,)),
            dma((chunks,)), dma((n // 2, chunks // 2)),
            dma((n // 2 - 1, chunks)), dma((chunks,)),
            dma((chunks,)), dma((chunks,)),
            dma((nb - 1,)), dma((nb - 1,)),
        ],
        compiler_params=pltpu.CompilerParams(collective_id=0, has_side_effects=True, vmem_limit_bytes=55168 * 1024),
    )(steering[0], estimates, spectra[0])
    updated, broadband = pl.pallas_call(
        store,
        out_shape=[jax.ShapeDtypeStruct((1, points), F32), jax.ShapeDtypeStruct((points,), F32)],
        in_specs=[pl.BlockSpec(memory_space=pltpu.VMEM)],
        out_specs=[pl.BlockSpec(memory_space=pltpu.VMEM)] * 2,
        compiler_params=pltpu.CompilerParams(vmem_limit_bytes=4 * 2**20),
    )(both)
    return updated, broadband


def solution(mesh):
    return jax.shard_map(
        functools.partial(body, mesh.shape["band"], mesh.shape["blk"]),
        mesh=mesh,
        in_specs=(P("blk", "band", None), P("blk", "band"), P("blk", "band", None)),
        out_specs=(P("blk", "band"), P("band")),
        check_vma=False,
    )
```
